128 devices in a mesh: grp: 8 (over y, core), aux: 16 (over x, z).
Axes of the slice: x: 4, y: 4, z: 4, core: 2. Of those that a mesh axis runs over, the one named last changes fastest.
Arguments:
- integral_tiles: bfloat16 [8, 16, 12, 32, 128, 128], P('grp', 'aux'), may hold values from -6 to 6
- row_blocks: int32 [8, 16, 12], P('grp', 'aux'), may hold values from 0 to 31
- col_blocks: int32 [8, 16, 12], P('grp', 'aux'), may hold values from 0 to 3
- aux_blocks: int32 [8, 16, 12], P('grp', 'aux'), may hold values from 0 to 15
- tile_counts: int32 [8, 16], P('grp', 'aux'), may hold values from 1 to 12, as said below
- occ_coeffs: bfloat16 [8, 4096], P(None, 'grp'), may hold values from -0.5 to 0.5
- vir_coeffs: bfloat16 [4096, 1024], P('grp'), may hold values from -0.5 to 0.5
Outputs:
- pair_factors: float32 [8192, 8192], P(('grp', 'aux'))
The draws below stay inside these ranges and needn't reach their ends.
Inputs may be any that keep to these rules, and one draw needn't show every extreme that they name: `tile_counts`: tile counts of the devices; some device holds exactly 12 kept tiles.
All inputs are finite; a program needn't handle non-finite values.
Results may differ from the reference program's by a relative error of at most 0.0029.
Values may be sent and summed in bfloat16 or wider, within the bound.
A program may use at most 128 MiB of HBM per device.

```python
import jax
import jax.numpy as jnp
from jax import lax

O = 8
V = 1024
BLK = 128
PB = 32
NBG = 4
PDEV = 512
KMAX = 12
NAO = 4096
NAUX = 8192
N_GRP = 8
N_AUX = 16


def draw_tile_counts(key, part):
    first_key, second_key = jax.random.split(jax.random.fold_in(key, 7))
    base = jax.random.randint(first_key, (N_GRP * N_AUX,), 1, KMAX + 1)
    chosen = jax.random.randint(second_key, (), 0, N_GRP * N_AUX)
    filled = jnp.where(jnp.arange(N_GRP * N_AUX) == chosen, KMAX, base)
    return filled.reshape(N_GRP, N_AUX).astype(jnp.int32)


def set_ends(entries, own_key, least, top_value):
    shape = entries.shape
    index_at = [jax.random.randint(jax.random.fold_in(own_key, axis), (), 0, shape[axis]) for axis in range(len(shape))]
    entries = entries.at[tuple(index_at)].set(least)
    longest = shape.index(max(shape))
    index_at[longest] = (index_at[longest] + 1) % shape[longest]
    return entries.at[tuple(index_at)].set(top_value)


def shard_levels(rng, extent, pieces, low, high):
    factor_of = 1.0
    for position, parts in pieces:
        draws = jax.random.uniform(jax.random.fold_in(jax.random.fold_in(rng, 6), position), (parts,), jnp.float32, low / len(pieces), high / len(pieces))
        factor_of = factor_of * jnp.repeat(jnp.exp(draws), extent[position] // parts).reshape((-1,) + (1,) * (len(extent) - 1 - position))
    return factor_of


def centred(stream_key, shape, width, most, pieces=(), held_as=jnp.bfloat16):
    loudness = shard_levels(stream_key, shape, pieces, -0.22, 0.18) if pieces else 1.0
    drawn = jax.random.normal(stream_key, shape, jnp.float32) * width * loudness
    return jnp.minimum(jnp.maximum(drawn, -most), most).astype(held_as)


def setup_inputs(seed: int = 0) -> dict:
    arg_keys = jax.random.split(jax.random.key(seed), 8)
    return {
        "integral_tiles": centred(arg_keys[0], (N_GRP, N_AUX, KMAX, PB, BLK, BLK), 1.0, 6.0, ((0, 8), (1, 16))),
        "row_blocks": set_ends(jax.random.randint(arg_keys[1], (N_GRP, N_AUX, KMAX), 0, NBG * N_GRP), jax.random.fold_in(arg_keys[1], 1), 0, (NBG * N_GRP) - 1).astype(jnp.int32),
        "col_blocks": set_ends(jax.random.randint(arg_keys[2], (N_GRP, N_AUX, KMAX), 0, NBG), jax.random.fold_in(arg_keys[2], 1), 0, NBG - 1).astype(jnp.int32),
        "aux_blocks": set_ends(jax.random.randint(arg_keys[3], (N_GRP, N_AUX, KMAX), 0, PDEV // PB), jax.random.fold_in(arg_keys[3], 1), 0, (PDEV // PB) - 1).astype(jnp.int32),
        "tile_counts": draw_tile_counts(jax.random.fold_in(arg_keys[7], 71), 0),
        "occ_coeffs": centred(arg_keys[5], (O, NAO), BLK ** -0.5, 0.5, ((1, 8),)),
        "vir_coeffs": centred(arg_keys[6], (NAO, V), BLK ** -0.5, 0.5, ((0, 8),)),
    }


def reference(integral_tiles, row_blocks, col_blocks, aux_blocks, tile_counts, occ_coeffs, vir_coeffs):
    flat_tiles = integral_tiles.reshape(N_GRP * N_AUX * KMAX, PB, BLK, BLK)
    flat_rows = row_blocks.reshape(-1)
    flat_cols = col_blocks.reshape(-1)
    flat_aux = aux_blocks.reshape(-1)
    result = jnp.zeros((O * V, NAUX), jnp.float32)

    def step(slot, result):
        group = slot // (N_AUX * KMAX)
        column = (slot // KMAX) % N_AUX
        inner = slot % KMAX
        tile = flat_tiles[slot].astype(jnp.float32)
        occ_block = lax.dynamic_slice_in_dim(occ_coeffs, (flat_rows[slot] * BLK).astype(jnp.int32), BLK, 1).astype(jnp.float32)
        half_tile = jnp.einsum('im,pmn->ipn', occ_block, tile).astype(jnp.bfloat16).astype(jnp.float32)
        vir_start = ((group * NBG + flat_cols[slot]) * BLK).astype(jnp.int32)
        vir_block = lax.dynamic_slice_in_dim(vir_coeffs, vir_start, BLK, 0).astype(jnp.float32)
        term = jnp.einsum('na,ipn->iap', vir_block, half_tile).reshape(O * V, PB)
        keep = (inner < tile_counts[group, column]).astype(jnp.float32)
        start = (column * PDEV + flat_aux[slot] * PB).astype(jnp.int32)
        current = lax.dynamic_slice_in_dim(result, start, PB, 1)
        return lax.dynamic_update_slice_in_dim(result, current + keep * term, start, 1)

    return lax.fori_loop(0, N_GRP * N_AUX * KMAX, step, result)
```

```python
import functools

import jax
import jax.numpy as jnp
from jax import lax
from jax.experimental import pallas as pl
from jax.experimental.pallas import tpu as pltpu
from jax.sharding import PartitionSpec as P

O = 8
V = 1024
BLK = 128
PB = 32
PDEV = 512
KMAX = 12
G = 8
NZ = 4
CH = 4
CT = KMAX // CH
MESH = pl.DeviceIdType.MESH


def rcopy(src, dst, ssem, rsem, dev):
    return pltpu.make_async_remote_copy(
        src_ref=src, dst_ref=dst, send_sem=ssem, recv_sem=rsem, device_id=dev, device_id_type=MESH
    )


def where_am_i():
    g = lax.axis_index("grp")
    a = lax.axis_index("aux")
    return g, a, lax.div(g, 2), lax.rem(g, 2), lax.div(a, NZ), lax.rem(a, NZ)


def spread_kernel(
    rows_ref, tiles_ref, cols_ref, aux_ref, count_ref, occ_ref, vir_ref,
    h_ref, v_ref, m_ref,
    tile_v, occ_all, meta_own, stage, hbuf,
    tile_sem, own_sem,
    occ_ss, occ_rs, meta_ss, meta_rs, mx_sem,
    h_ss, h_rs, hx_ss, hx_rs,
    vy_ss, vy_rs, vz_ss, vz_rs, vo_ss, vo_rs, vs_ss, vs_rs,
):
    g, a, y, c, x, z = where_am_i()
    s = lax.rem(x, 2)
    mate = (g, (x + 1 - 2 * s) * NZ + z)
    twin = (2 * y + 1 - c, a)
    xb = (x, 3 - x)

    def tile_copy(k):
        return pltpu.make_async_copy(tiles_ref.at[k], tile_v.at[k], tile_sem.at[k])

    for k in range(KMAX):
        tile_copy(k).start()

    def vir_cols(j):
        return vir_ref.at[:, :, pl.ds(pl.multiple_of(xb[j] * 256, 256), 256)]

    v_own = [pltpu.make_async_copy(vir_cols(j), v_ref.at[g, :, j], own_sem.at[j]) for j in range(2)]
    for cp in v_own:
        cp.start()

    for b in range(4):
        occ_all[g, b] = occ_ref[:, b * BLK:(b + 1) * BLK]
    meta_own[...] = jnp.zeros_like(meta_own)
    meta_own[0:1, 0:KMAX] = cols_ref[...]
    meta_own[1:2, 0:KMAX] = aux_ref[...]
    meta_own[2:3, 0:1] = count_ref[...]
    m_own = pltpu.make_async_copy(meta_own, m_ref.at[s, g], own_sem.at[2])
    m_own.start()

    peers = [lax.rem(g + d, G) for d in range(1, G)]
    ypeers = [2 * lax.rem(y + d, 4) + c for d in range(1, 4)]
    zpeers = [lax.rem(z + d, NZ) for d in range(1, NZ)]

    barrier = pltpu.get_barrier_semaphore()
    for p in peers:
        pl.semaphore_signal(barrier, inc=1, device_id=(p, a), device_id_type=MESH)
    pl.semaphore_signal(barrier, inc=1, device_id=mate, device_id_type=MESH)
    for zp in zpeers:
        pl.semaphore_signal(barrier, inc=1, device_id=(g, x * NZ + zp), device_id_type=MESH)
    pl.semaphore_wait(barrier, 11)

    def occ_copy(src, d, dev):
        return rcopy(occ_all.at[src], occ_all.at[src], occ_ss.at[d], occ_rs.at[src], dev)

    def meta_copy(src, d, dev):
        return rcopy(meta_own, m_ref.at[s, src], meta_ss.at[d], meta_rs.at[src], dev)

    for d, p in enumerate(peers):
        occ_copy(g, d, (p, a)).start()

    def vy_copy(src, d, j, dev):
        return rcopy(
            vir_ref.at[z, :, pl.ds(pl.multiple_of(xb[j] * 256, 256), 256)],
            v_ref.at[src, z, j], vy_ss.at[d, j], vy_rs.at[lax.div(src, 2), j], dev,
        )

    for d, p in enumerate(ypeers):
        for j in range(2):
            vy_copy(g, d, j, (p, a)).start()
    for d, p in enumerate(peers):
        meta_copy(g, d, (p, a)).start()

    def vo_copy(src, j):
        return rcopy(vir_cols(j), v_ref.at[src, :, j], vo_ss.at[j], vo_rs.at[j], twin)

    for j in range(2):
        vo_copy(g, j).start()

    for d, p in enumerate(peers):
        occ_copy(p, d, (p, a)).wait_recv()

    def compute(chunk):
        def one(t, carry):
            k = chunk * CT + t
            tile_copy(k).wait()
            row = rows_ref[k]
            occ = occ_all[lax.div(row, 4), lax.rem(row, 4)]
            for pp in range(PB // 2):
                rhs = jnp.concatenate([tile_v[k, 2 * pp], tile_v[k, 2 * pp + 1]], axis=1)
                out = jnp.dot(occ, rhs, preferred_element_type=jnp.float32)
                stage[16 * pp:16 * pp + 8, :] = out[:, :BLK]
                stage[16 * pp + 8:16 * pp + 16, :] = out[:, BLK:]
            for i in range(O):
                hbuf[i, chunk, t] = stage[pl.ds(i, PB, stride=O), :].astype(jnp.bfloat16)
            return carry

        lax.fori_loop(0, CT, one, 0)

    def h_copy(dst_g, src, chunk, d, dev):
        return rcopy(
            hbuf.at[dst_g, chunk], h_ref.at[s, chunk, src], h_ss.at[chunk, d], h_rs.at[chunk, src], dev
        )

    def h_own(chunk):
        return pltpu.make_async_copy(hbuf.at[g, chunk], h_ref.at[s, chunk, g], own_sem.at[3 + chunk])

    def hx_copy(side, chunk):
        return rcopy(h_ref.at[side, chunk], h_ref.at[side, chunk], hx_ss.at[chunk], hx_rs.at[chunk], mate)

    def mx_copy(side):
        return rcopy(m_ref.at[side], m_ref.at[side], mx_sem.at[0], mx_sem.at[1], mate)

    def forward_h(chunk):
        h_own(chunk).wait()
        for d, p in enumerate(peers):
            h_copy(p, p, chunk, d, (p, a)).wait_recv()
        hx_copy(s, chunk).start()

    def vz_copy(src, src_z, d, e, dev):
        return rcopy(
            v_ref.at[src, src_z], v_ref.at[src, src_z], vz_ss.at[d, e],
            vz_rs.at[lax.div(src, 2), src_z], dev,
        )

    def vs_copy(src, d):
        return rcopy(v_ref.at[src], v_ref.at[src], vs_ss.at[d], vs_rs.at[lax.div(src, 2)], twin)

    for chunk in range(CH):
        compute(chunk)
        for d, p in enumerate(peers):
            h_copy(p, g, chunk, d, (p, a)).start()
        h_own(chunk).start()
        if chunk == 0:
            for d, p in enumerate(ypeers):
                for j in range(2):
                    vy_copy(p, d, j, (p, a)).wait_recv()
                for e, zp in enumerate(zpeers):
                    vz_copy(p, z, d, e, (g, x * NZ + zp)).start()
        if chunk == 1:
            m_own.wait()
            for d, p in enumerate(peers):
                meta_copy(p, d, (p, a)).wait_recv()
            mx_copy(s).start()
        if chunk >= 1:
            forward_h(chunk - 1)
    forward_h(CH - 1)
    for d, p in enumerate(ypeers):
        for e, zp in enumerate(zpeers):
            vz_copy(p, zp, d, e, (g, x * NZ + zp)).wait_recv()
        vs_copy(p, d).start()

    for j in range(2):
        vo_copy(2 * y + 1 - c, j).wait_recv()
        v_own[j].wait()
    mx_copy(1 - s).wait_recv()
    for chunk in range(CH):
        hx_copy(1 - s, chunk).wait_recv()
    for d in range(1, 4):
        vs_copy(2 * lax.rem(y + d, 4) + 1 - c, d - 1).wait_recv()

    for d, p in enumerate(peers):
        occ_copy(g, d, (p, a)).wait_send()
        meta_copy(g, d, (p, a)).wait_send()
        for chunk in range(CH):
            h_copy(p, g, chunk, d, (p, a)).wait_send()
    for d, p in enumerate(ypeers):
        for j in range(2):
            vy_copy(g, d, j, (p, a)).wait_send()
        for e, zp in enumerate(zpeers):
            vz_copy(p, z, d, e, (g, x * NZ + zp)).wait_send()
        vs_copy(p, d).wait_send()
    for j in range(2):
        vo_copy(g, j).wait_send()
    mx_copy(s).wait_send()
    for chunk in range(CH):
        hx_copy(s, chunk).wait_send()


def spread(rows, tiles, cols, aux, count, occ, vir):
    any_spec = pl.BlockSpec(memory_space=pl.ANY)
    vmem = pl.BlockSpec(memory_space=pltpu.VMEM)
    dma = pltpu.SemaphoreType.DMA
    return pl.pallas_call(
        spread_kernel,
        out_shape=(
            jax.ShapeDtypeStruct((2, CH, G, CT, PB, BLK), jnp.bfloat16),
            jax.ShapeDtypeStruct((G, 4, 2, BLK, 256), jnp.bfloat16),
            jax.ShapeDtypeStruct((2, G, 8, 128), jnp.int32),
        ),
        in_specs=[pl.BlockSpec(memory_space=pltpu.SMEM), any_spec, vmem, vmem, vmem, vmem, any_spec],
        out_specs=(any_spec, any_spec, any_spec),
        scratch_shapes=[
            pltpu.VMEM((KMAX, PB, BLK, BLK), jnp.bfloat16),
            pltpu.VMEM((G, 4, O, BLK), jnp.bfloat16),
            pltpu.VMEM((8, 128), jnp.int32),
            pltpu.VMEM((PB * O, BLK), jnp.float32),
            pltpu.VMEM((O, CH, CT, PB, BLK), jnp.bfloat16),
            dma((KMAX,)), dma((3 + CH,)),
            dma((7,)), dma((G,)), dma((7,)), dma((G,)), dma((2,)),
            dma((CH, 7)), dma((CH, G)), dma((CH,)), dma((CH,)),
            dma((3, 2)), dma((4, 2)), dma((3, 3)), dma((4, NZ)),
            dma((2,)), dma((2,)), dma((3,)), dma((4,)),
        ],
        compiler_params=pltpu.CompilerParams(
            collective_id=0, has_side_effects=True, vmem_limit_bytes=40 * 1024 * 1024
        ),
        name="spread",
    )(rows, tiles, cols, aux, count, occ, vir)


UN = 6


def contract_kernel(m_ref, h_ref, v_ref, out_ref, acc):
    s = pl.program_id(0)
    acc[...] = jnp.zeros_like(acc)

    def group(g, carry):
        count = m_ref[s, g, 2, 0]
        for part in range(KMAX // UN):
            @pl.when(count > part * UN)
            def _():
                for t in range(UN):
                    k = part * UN + t
                    col = m_ref[s, g, 0, k]
                    start = pl.multiple_of(m_ref[s, g, 1, k] * PB, PB)
                    half = h_ref[0, k // CT, g, k % CT]
                    half = jnp.where(k < count, half, jnp.zeros_like(half))
                    for j in range(2):
                        term = jnp.dot(half, v_ref[g, col, j], preferred_element_type=jnp.float32)
                        acc[j, pl.ds(start, PB), :] += term
        return carry

    lax.fori_loop(0, G, group, 0)
    for j in range(2):
        out_ref[0, j * 256:(j + 1) * 256, :] = acc[j].T.astype(jnp.bfloat16)


def contract(meta, halves, vir):
    return pl.pallas_call(
        contract_kernel,
        out_shape=jax.ShapeDtypeStruct((2, 512, PDEV), jnp.bfloat16),
        grid_spec=pltpu.PrefetchScalarGridSpec(
            num_scalar_prefetch=1,
            grid=(2,),
            in_specs=[
                pl.BlockSpec((1, CH, G, CT, PB, BLK), lambda s, m: (s, 0, 0, 0, 0, 0)),
                pl.BlockSpec((G, 4, 2, BLK, 256), lambda s, m: (0, 0, 0, 0, 0)),
            ],
            out_specs=pl.BlockSpec((1, 512, PDEV), lambda s, m: (s, 0, 0)),
            scratch_shapes=[pltpu.VMEM((2, PDEV, 256), jnp.float32)],
        ),
        compiler_params=pltpu.CompilerParams(vmem_limit_bytes=40 * 1024 * 1024),
        name="contract",
    )(meta, halves, vir)


def deliver_kernel(r_ref, o_ref, own_sem, ss, rs):
    g, a, y, c, x, z = where_am_i()
    s = lax.rem(x, 2)
    xb = (x, 3 - x)
    dests = [(j, lax.rem(z + d, NZ), d) for d in range(NZ) for j in range(2) if (d, j) != (0, 0)]

    barrier = pltpu.get_barrier_semaphore()
    for j, zp, d in dests:
        pl.semaphore_signal(barrier, inc=1, device_id=(g, xb[j] * NZ + zp), device_id_type=MESH)

    def columns(x_src, z_src, side):
        first = ((x_src - lax.rem(x_src, 2) + side) * NZ + z_src) * PDEV
        return o_ref.at[:, pl.ds(pl.multiple_of(first, PDEV), PDEV)]

    def piece(j, zp, side):
        return r_ref.at[side, pl.ds(pl.multiple_of(j * 256 + zp * 64, 64), 64), :]

    own = [pltpu.make_async_copy(piece(0, z, t), columns(x, z, t), own_sem.at[t]) for t in range(2)]
    for cp in own:
        cp.start()
    pl.semaphore_wait(barrier, len(dests))

    for j, zp, d in dests:
        for t in range(2):
            rcopy(
                piece(j, zp, t), columns(x, z, t), ss.at[j, d, t], rs.at[j, z, t], (g, xb[j] * NZ + zp)
            ).start()
    for j, zp, d in dests:
        for t in range(2):
            rcopy(
                piece(j, zp, t), columns(xb[j], zp, t), ss.at[j, d, t], rs.at[j, zp, t],
                (g, xb[j] * NZ + zp),
            ).wait_recv()
    for cp in own:
        cp.wait()
    for j, zp, d in dests:
        for t in range(2):
            rcopy(
                piece(j, zp, t), columns(x, z, t), ss.at[j, d, t], rs.at[j, z, t], (g, xb[j] * NZ + zp)
            ).wait_send()


def deliver(finished):
    dma = pltpu.SemaphoreType.DMA
    return pl.pallas_call(
        deliver_kernel,
        out_shape=jax.ShapeDtypeStruct((64, 16 * PDEV), jnp.bfloat16),
        in_specs=[pl.BlockSpec(memory_space=pl.ANY)],
        out_specs=pl.BlockSpec(memory_space=pl.ANY),
        scratch_shapes=[dma((2,)), dma((2, NZ, 2)), dma((2, NZ, 2))],
        compiler_params=pltpu.CompilerParams(collective_id=1, has_side_effects=True),
        name="deliver",
    )(finished)


def shards(integral_tiles, row_blocks, col_blocks, aux_blocks, tile_counts, occ_coeffs, vir_coeffs):
    halves, vir, meta = spread(
        row_blocks.reshape(KMAX),
        integral_tiles.reshape(KMAX, PB, BLK, BLK),
        col_blocks.reshape(1, KMAX),
        aux_blocks.reshape(1, KMAX),
        tile_counts,
        occ_coeffs,
        vir_coeffs.reshape(4, BLK, V),
    )
    finished = contract(meta, halves, vir)
    return deliver(finished).astype(jnp.float32)


def solution(mesh):
    in_specs = (
        P("grp", "aux", None, None, None, None),
        P("grp", "aux", None),
        P("grp", "aux", None),
        P("grp", "aux", None),
        P("grp", "aux"),
        P(None, "grp"),
        P("grp", None),
    )
    out_specs = P(("grp", "aux"), None)
    return jax.shard_map(shards, mesh=mesh, in_specs=in_specs, out_specs=out_specs, check_vma=False)
```

```python
import functools

import jax
import jax.numpy as jnp
from jax import lax
from jax.experimental import pallas as pl
from jax.experimental.pallas import tpu as pltpu
from jax.sharding import PartitionSpec as P

O = 8
V = 1024
BLK = 128
PB = 32
PDEV = 512
KMAX = 12
G = 8
NZ = 4
CH = 4
CT = KMAX // CH
MESH = pl.DeviceIdType.MESH


def rcopy(src, dst, ssem, rsem, dev):
    return pltpu.make_async_remote_copy(
        src_ref=src, dst_ref=dst, send_sem=ssem, recv_sem=rsem, device_id=dev, device_id_type=MESH
    )


def where_am_i():
    g = lax.axis_index("grp")
    a = lax.axis_index("aux")
    return g, a, lax.div(g, 2), lax.rem(g, 2), lax.div(a, NZ), lax.rem(a, NZ)


def mate_x(x, c):
    odd = lax.rem(x, 2)
    return lax.rem(x + 4 + (1 - 2 * odd) * (1 - 2 * c), 4)


def whole_kernel(
    rows_ref, tiles_ref, cols_ref, aux_ref, count_ref, occ_ref, vir_ref,
    o_ref,
    h_ref, v_ref, m_ref, run, done, tab_v, tab,
    rows_s, cols_v, aux_v, count_v, occ_v, tile_v, occ_all, meta_own, stage, hbuf,
    in_sem, tile_sem, own_sem,
    occ_ss, occ_rs, meta_ss, meta_rs, mx_sem,
    h_ss, h_rs, hx_ss, hx_rs,
    vy_ss, vy_rs, vz_ss, vz_rs, vf_ss, vf_rs, vo_ss, vo_rs, vs_ss, vs_rs,
    tab_sem, o_own, o_ss, o_rs,
):
    g, a, y, c, x, z = where_am_i()
    xm = mate_x(x, c)
    mate = (g, xm * NZ + z)
    twin = (2 * y + 1 - c, a)
    xb = (x, lax.rem(x + 2, 4))

    small = [
        pltpu.make_async_copy(src, dst, in_sem.at[n])
        for n, (src, dst) in enumerate((
            (occ_ref, occ_v), (cols_ref, cols_v), (aux_ref, aux_v), (count_ref, count_v), (rows_ref, rows_s)
        ))
    ]
    for cp in small:
        cp.start()

    peers = [lax.rem(g + d, G) for d in range(1, G)]
    ypeers = [2 * lax.rem(y + d, 4) + c for d in (1, 3, 2)]
    zpeers = [lax.rem(z + d, NZ) for d in (1, 3)]
    far_z = lax.rem(z + 2, NZ)
    dests = [(j, lax.rem(z + d, NZ), d) for d in range(NZ) for j in range(2) if (d, j) != (0, 0)]

    barrier = pltpu.get_barrier_semaphore()
    for p in peers:
        pl.semaphore_signal(barrier, inc=1, device_id=(p, a), device_id_type=MESH)
    pl.semaphore_signal(barrier, inc=1, device_id=mate, device_id_type=MESH)
    for j, zp, d in dests:
        pl.semaphore_signal(barrier, inc=1, device_id=(g, xb[j] * NZ + zp), device_id_type=MESH)

    def tile_copy(k):
        return pltpu.make_async_copy(tiles_ref.at[k], tile_v.at[k], tile_sem.at[k])

    for k in range(KMAX):
        tile_copy(k).start()

    def vir_cols(j):
        return vir_ref.at[:, :, pl.ds(pl.multiple_of(xb[j] * 256, 256), 256)]

    v_own = [pltpu.make_async_copy(vir_cols(j), v_ref.at[g, :, j], own_sem.at[j]) for j in range(2)]
    for cp in v_own:
        cp.start()

    for cp in small:
        cp.wait()
    for b in range(4):
        occ_all[g, b] = occ_v[:, b * BLK:(b + 1) * BLK]
    meta_own[...] = jnp.zeros_like(meta_own)
    kept = lax.broadcasted_iota(jnp.int32, (1, KMAX), 1) < count_v[...]
    meta_own[0:1, 0:KMAX] = jnp.where(kept, aux_v[...] + 1, 0)
    meta_own[1:2, 0:KMAX] = cols_v[...]
    meta_own[...] = pltpu.roll(meta_own[...], KMAX * g, 1)
    m_own = pltpu.make_async_copy(meta_own, m_ref.at[0, g], own_sem.at[2])
    m_own.start()

    pl.semaphore_wait(barrier, 8 + len(dests))

    def occ_copy(src, d, dev):
        return rcopy(occ_all.at[src], occ_all.at[src], occ_ss.at[d], occ_rs.at[src], dev)

    def meta_copy(src, d, dev):
        return rcopy(meta_own, m_ref.at[0, src], meta_ss.at[d], meta_rs.at[src], dev)

    for d, p in enumerate(peers):
        occ_copy(g, d, (p, a)).start()

    def vy_copy(src, d, j, dev):
        return rcopy(
            vir_ref.at[z, :, pl.ds(pl.multiple_of(xb[j] * 256, 256), 256)],
            v_ref.at[src, z, j], vy_ss.at[d, j], vy_rs.at[lax.div(src, 2), j], dev,
        )

    for d, p in enumerate(ypeers):
        for j in range(2):
            vy_copy(g, d, j, (p, a)).start()
    for d, p in enumerate(peers):
        meta_copy(g, d, (p, a)).start()

    def vo_copy(src, j):
        return rcopy(vir_cols(j), v_ref.at[src, :, j], vo_ss.at[j], vo_rs.at[j], twin)

    for j in range(2):
        vo_copy(g, j).start()

    for d, p in enumerate(peers):
        occ_copy(p, d, (p, a)).wait_recv()

    def compute(chunk):
        def one(t, carry):
            k = chunk * CT + t
            tile_copy(k).wait()
            row = rows_s[0, k]
            occ = occ_all[lax.div(row, 4), lax.rem(row, 4)]
            for pp in range(PB // 2):
                rhs = jnp.concatenate([tile_v[k, 2 * pp], tile_v[k, 2 * pp + 1]], axis=1)
                out = jnp.dot(occ, rhs, preferred_element_type=jnp.float32)
                stage[16 * pp:16 * pp + 8, :] = out[:, :BLK]
                stage[16 * pp + 8:16 * pp + 16, :] = out[:, BLK:]
            for i in range(O):
                hbuf[i, chunk, t] = stage[pl.ds(i, PB, stride=O), :].astype(jnp.bfloat16)
            return carry

        lax.fori_loop(0, CT, one, 0)

    def h_copy(dst_g, src, chunk, d, dev):
        return rcopy(
            hbuf.at[dst_g, chunk], h_ref.at[0, chunk, src], h_ss.at[chunk, d], h_rs.at[chunk, src], dev
        )

    def h_own(chunk):
        return pltpu.make_async_copy(hbuf.at[g, chunk], h_ref.at[0, chunk, g], own_sem.at[3 + chunk])

    def hx_copy(chunk):
        return rcopy(h_ref.at[0, chunk], h_ref.at[1, chunk], hx_ss.at[chunk], hx_rs.at[chunk], mate)

    def mx_copy():
        return rcopy(m_ref.at[0], m_ref.at[1], mx_sem.at[0], mx_sem.at[1], mate)

    def forward_h(chunk):
        h_own(chunk).wait()
        for d, p in enumerate(peers):
            h_copy(p, p, chunk, d, (p, a)).wait_recv()
        hx_copy(chunk).start()

    def vz_copy(src, src_z, d, e, dev):
        return rcopy(
            v_ref.at[src, src_z], v_ref.at[src, src_z], vz_ss.at[d, e],
            vz_rs.at[lax.div(src, 2), src_z], dev,
        )

    def vf_copy(src, src_z, d, e, dev):
        return rcopy(
            v_ref.at[src, src_z, e], v_ref.at[src, src_z, e], vf_ss.at[d, e],
            vf_rs.at[lax.div(src, 2), e], dev,
        )

    def vs_copy(src, d):
        return rcopy(v_ref.at[src], v_ref.at[src], vs_ss.at[d], vs_rs.at[lax.div(src, 2)], twin)

    def start_z(d):
        p = ypeers[d]
        for j in range(2):
            vy_copy(p, d, j, (p, a)).wait_recv()
        for e, zp in enumerate(zpeers):
            vz_copy(p, z, d, e, (g, x * NZ + zp)).start()

    def pass_z(d):
        p = ypeers[d]
        for e in range(2):
            vz_copy(p, zpeers[1 - e], d, e, (g, x * NZ + zpeers[1 - e])).wait_recv()
            vf_copy(p, zpeers[1 - e], d, e, (g, x * NZ + zpeers[e])).start()

    def finish_z(d):
        p = ypeers[d]
        for e in range(2):
            vf_copy(p, far_z, d, e, (g, x * NZ + zpeers[e])).wait_recv()
        vs_copy(p, d).start()

    for chunk in range(CH):
        compute(chunk)
        for d, p in enumerate(peers):
            h_copy(p, g, chunk, d, (p, a)).start()
        h_own(chunk).start()
        if chunk == 1:
            start_z(0)
            start_z(1)
        if chunk == 2:
            start_z(2)
        if chunk == 3:
            m_own.wait()
            for d, p in enumerate(peers):
                meta_copy(p, d, (p, a)).wait_recv()
            mx_copy().start()
    forward_h(0)
    pass_z(0)
    forward_h(1)
    pass_z(1)
    forward_h(2)
    pass_z(2)
    forward_h(3)
    for d in range(3):
        finish_z(d)

    def chain(side):
        total = m_ref[side, 0]
        for p in range(1, G):
            total += m_ref[side, p]
        key = jnp.broadcast_to(total[0:1, :], (128, 128))
        key_t = key.T
        slot = lax.broadcasted_iota(jnp.int32, (128, 128), 0)
        lane = lax.broadcasted_iota(jnp.int32, (128, 128), 1)
        before = jnp.where((key_t == key) & (slot < lane), slot + 1, 0)
        last = jnp.where(key_t == lane + 1, slot + 1, 0)
        tab_v[side, 0:1, :] = jnp.max(before, axis=0, keepdims=True)
        tab_v[side, 1:2, :] = total[1:2, :]
        tab_v[side, 2:3, :] = jnp.max(last, axis=0, keepdims=True)
        return pltpu.make_async_copy(tab_v.at[side], tab.at[side], tab_sem.at[side])

    def contract(side):
        def group(p, carry):
            for k in range(KMAX):
                t = p * KMAX + k
                col = tab[side, 1, t]
                prev = tab[side, 0, t]
                half = h_ref[side, k // CT, p, k % CT]
                for j in range(2):
                    term = jnp.dot(half, v_ref[p, col, j], preferred_element_type=jnp.float32)
                    run[t + 1, j] = term + run[prev, j]
            return carry

        lax.fori_loop(0, G, group, 0)

        def flip(q, carry):
            at = [tab[side, 2, 4 * q + b] for b in range(4)]
            for j in range(2):
                block = jnp.concatenate([run[at[b], j] for b in range(4)], axis=0)
                done[side, q, j] = block.T.astype(jnp.bfloat16)
            return carry

        lax.fori_loop(0, PDEV // BLK, flip, 0)

    def columns(x_src, z_src, side, q):
        x_aux = (x_src, mate_x(x_src, c))[side]
        first = (x_aux * NZ + z_src) * PDEV + q * BLK
        return o_ref.at[:, pl.ds(pl.multiple_of(first, BLK), BLK)]

    def piece(j, zp, side, q):
        return done.at[side, q, j, pl.ds(pl.multiple_of(zp * 64, 64), 64), :]

    def out_copy(j, zp, d, side, q, x_src, z_src):
        return rcopy(
            piece(j, zp, side, q), columns(x_src, z_src, side, q), o_ss.at[j, d, side, q],
            o_rs.at[j, z_src, side, q], (g, xb[j] * NZ + zp),
        )

    def own_copy(side, q):
        return pltpu.make_async_copy(piece(0, z, side, q), columns(x, z, side, q), o_own.at[side, q])

    def send_out(side):
        for j, zp, d in dests:
            for q in range(4):
                out_copy(j, zp, d, side, q, x, z).start()
        for q in range(4):
            own_copy(side, q).start()

    for j in range(2):
        vo_copy(2 * y + 1 - c, j).wait_recv()
        v_own[j].wait()
    mx_copy().wait_recv()
    tables = [chain(side) for side in range(2)]
    for cp in tables:
        cp.start()
    run[0] = jnp.zeros_like(run[0])
    for cp in tables:
        cp.wait()
    for d in range(1, 4):
        vs_copy(2 * lax.rem(y + d, 4) + 1 - c, d - 1).wait_recv()
    contract(0)
    send_out(0)
    for chunk in range(CH):
        hx_copy(chunk).wait_recv()
    contract(1)
    send_out(1)

    for side in range(2):
        for j, zp, d in dests:
            for q in range(4):
                out_copy(j, zp, d, side, q, xb[j], zp).wait_recv()
        for q in range(4):
            own_copy(side, q).wait()
    for side in range(2):
        for j, zp, d in dests:
            for q in range(4):
                out_copy(j, zp, d, side, q, x, z).wait_send()

    for d, p in enumerate(peers):
        occ_copy(g, d, (p, a)).wait_send()
        meta_copy(g, d, (p, a)).wait_send()
        for chunk in range(CH):
            h_copy(p, g, chunk, d, (p, a)).wait_send()
    for d, p in enumerate(ypeers):
        for j in range(2):
            vy_copy(g, d, j, (p, a)).wait_send()
        for e in range(2):
            vz_copy(p, z, d, e, (g, x * NZ + zpeers[e])).wait_send()
            vf_copy(p, zpeers[1 - e], d, e, (g, x * NZ + zpeers[e])).wait_send()
        vs_copy(p, d).wait_send()
    for j in range(2):
        vo_copy(g, j).wait_send()
    mx_copy().wait_send()
    for chunk in range(CH):
        hx_copy(chunk).wait_send()


def whole(rows, tiles, cols, aux, count, occ, vir):
    anywhere = pl.BlockSpec(memory_space=pl.ANY)
    dma = pltpu.SemaphoreType.DMA
    return pl.pallas_call(
        whole_kernel,
        out_shape=jax.ShapeDtypeStruct((64, 16 * PDEV), jnp.bfloat16),
        in_specs=[anywhere] * 7,
        out_specs=anywhere,
        scratch_shapes=[
            pltpu.VMEM((2, CH, G, CT, PB, BLK), jnp.bfloat16),
            pltpu.VMEM((G, 4, 2, BLK, 256), jnp.bfloat16),
            pltpu.VMEM((2, G, 8, 128), jnp.int32),
            pltpu.VMEM((1 + G * KMAX, 2, PB, 256), jnp.float32),
            pltpu.VMEM((2, 4, 2, 256, BLK), jnp.bfloat16),
            pltpu.VMEM((2, 8, 128), jnp.int32),
            pltpu.SMEM((2, 8, 128), jnp.int32),
            pltpu.SMEM((1, KMAX), jnp.int32),
            pltpu.VMEM((1, KMAX), jnp.int32),
            pltpu.VMEM((1, KMAX), jnp.int32),
            pltpu.VMEM((1, 1), jnp.int32),
            pltpu.VMEM((O, 4 * BLK), jnp.bfloat16),
            pltpu.VMEM((KMAX, PB, BLK, BLK), jnp.bfloat16),
            pltpu.VMEM((G, 4, O, BLK), jnp.bfloat16),
            pltpu.VMEM((8, 128), jnp.int32),
            pltpu.VMEM((PB * O, BLK), jnp.float32),
            pltpu.VMEM((O, CH, CT, PB, BLK), jnp.bfloat16),
            dma((5,)), dma((KMAX,)), dma((3 + CH,)),
            dma((7,)), dma((G,)), dma((7,)), dma((G,)), dma((2,)),
            dma((CH, 7)), dma((CH, G)), dma((CH,)), dma((CH,)),
            dma((3, 2)), dma((4, 2)), dma((3, 2)), dma((4, NZ)), dma((3, 2)), dma((4, 2)),
            dma((2,)), dma((2,)), dma((3,)), dma((4,)),
            dma((2,)), dma((2, 4)), dma((2, NZ, 2, 4)), dma((2, NZ, 2, 4)),
        ],
        compiler_params=pltpu.CompilerParams(
            collective_id=0, has_side_effects=True, vmem_limit_bytes=60 * 1024 * 1024
        ),
        name="whole",
    )(rows, tiles, cols, aux, count, occ, vir)


def shards(integral_tiles, row_blocks, col_blocks, aux_blocks, tile_counts, occ_coeffs, vir_coeffs):
    result = whole(
        row_blocks.reshape(1, KMAX),
        integral_tiles.reshape(KMAX, PB, BLK, BLK),
        col_blocks.reshape(1, KMAX),
        aux_blocks.reshape(1, KMAX),
        tile_counts,
        occ_coeffs,
        vir_coeffs.reshape(4, BLK, V),
    )
    return result.astype(jnp.float32)


def solution(mesh):
    in_specs = (
        P("grp", "aux", None, None, None, None),
        P("grp", "aux", None),
        P("grp", "aux", None),
        P("grp", "aux", None),
        P("grp", "aux"),
        P(None, "grp"),
        P("grp", None),
    )
    out_specs = P(("grp", "aux"), None)
    return jax.shard_map(shards, mesh=mesh, in_specs=in_specs, out_specs=out_specs, check_vma=False)
```

```python
import functools

import jax
import jax.numpy as jnp
from jax import lax
from jax.experimental import pallas as pl
from jax.experimental.pallas import tpu as pltpu
from jax.sharding import PartitionSpec as P

O = 8
V = 1024
BLK = 128
PB = 32
PDEV = 512
KMAX = 12
G = 8
NZ = 4
CH = 4
CT = KMAX // CH
MESH = pl.DeviceIdType.MESH


def rcopy(src, dst, ssem, rsem, dev):
    return pltpu.make_async_remote_copy(
        src_ref=src, dst_ref=dst, send_sem=ssem, recv_sem=rsem, device_id=dev, device_id_type=MESH
    )


def where_am_i():
    g = lax.axis_index("grp")
    a = lax.axis_index("aux")
    return g, a, lax.div(g, 2), lax.rem(g, 2), lax.div(a, NZ), lax.rem(a, NZ)


def mate_x(x, c):
    odd = lax.rem(x, 2)
    return lax.rem(x + 4 + (1 - 2 * odd) * (1 - 2 * c), 4)


def whole_kernel(
    rows_ref, tiles_ref, cols_ref, aux_ref, count_ref, occ_ref, vir_ref,
    o_ref,
    h_ref, vf_ref, vn_ref, m_ref, run, done, tab_v, tab,
    rows_s, cols_v, aux_v, count_v, occ_v, tile_v, occ_all, meta_own, stage, hbuf,
    in_sem, tile_sem, own_sem,
    occ_ss, occ_rs, meta_ss, meta_rs, mx_sem,
    h_ss, h_rs, hx_ss, hx_rs,
    vy_ss, vy_rs, vz_ss, vz_rs, zf_ss, zf_rs, vo_ss, vo_rs, vs_ss, vs_rs,
    tab_sem, o_own, o_ss, o_rs, ready,
):
    g, a, y, c, x, z = where_am_i()
    xm = mate_x(x, c)
    mate = (g, xm * NZ + z)
    twin = (2 * y + 1 - c, a)
    xb = (lax.rem(x + 2, 4), x)
    v_ref = (vf_ref, vn_ref)

    small = [
        pltpu.make_async_copy(src, dst, in_sem.at[n])
        for n, (src, dst) in enumerate((
            (occ_ref, occ_v), (cols_ref, cols_v), (aux_ref, aux_v), (count_ref, count_v), (rows_ref, rows_s)
        ))
    ]
    for cp in small:
        cp.start()

    peers = [2 * lax.rem(y + d, 4) + lax.rem(c + e, 2) for d, e in ((0, 1), (1, 0), (3, 0), (1, 1), (3, 1), (2, 0), (2, 1))]
    around = [2 * lax.rem(y + d, 4) + c for d in range(4)]
    quarter = [lax.rem(z + d, NZ) for d in range(4)]
    block = (around[3], around[1], around[2])
    ahead = (1, 3)
    dests = [(j, quarter[d], d) for j in range(2) for d in range(NZ) if (d, j) != (0, 1)]

    barrier = pltpu.get_barrier_semaphore()
    for p in peers:
        pl.semaphore_signal(barrier, inc=1, device_id=(p, a), device_id_type=MESH)
    below = (g, lax.rem(x + 3, 4) * NZ + z)
    above = (g, lax.rem(x + 1, 4) * NZ + z)
    for dev in (below, above):
        pl.semaphore_signal(barrier, inc=1, device_id=dev, device_id_type=MESH)
    for zp in quarter[1:]:
        pl.semaphore_signal(barrier, inc=1, device_id=(g, x * NZ + zp), device_id_type=MESH)

    def tile_copy(k):
        return pltpu.make_async_copy(tiles_ref.at[k], tile_v.at[k], tile_sem.at[k])

    for k in range(KMAX):
        tile_copy(k).start()

    def vir_cols(j):
        return vir_ref.at[:, :, pl.ds(pl.multiple_of(xb[j] * 256, 256), 256)]

    v_own = [pltpu.make_async_copy(vir_cols(j), v_ref[j].at[g], own_sem.at[j]) for j in range(2)]
    for cp in v_own:
        cp.start()

    for cp in small:
        cp.wait()
    for b in range(4):
        occ_all[g, b] = occ_v[:, b * BLK:(b + 1) * BLK]
    meta_own[...] = jnp.zeros_like(meta_own)
    kept = lax.broadcasted_iota(jnp.int32, (1, KMAX), 1) < count_v[...]
    meta_own[0:1, 0:KMAX] = jnp.where(kept, aux_v[...] + 1, 0)
    meta_own[1:2, 0:KMAX] = cols_v[...]
    meta_own[...] = pltpu.roll(meta_own[...], KMAX * g, 1)
    m_own = pltpu.make_async_copy(meta_own, m_ref.at[0, g], own_sem.at[2])
    m_own.start()

    pl.semaphore_wait(barrier, 12)
    pl.semaphore_signal(ready.at[0], inc=1, device_id=below, device_id_type=MESH)

    def occ_copy(src, d, dev):
        return rcopy(occ_all.at[src], occ_all.at[src], occ_ss.at[d], occ_rs.at[src], dev)

    def meta_copy(src, d, dev):
        return rcopy(meta_own, m_ref.at[0, src], meta_ss.at[d], meta_rs.at[src], dev)

    for d, p in enumerate(peers):
        occ_copy(g, d, (p, a)).start()

    def vy_copy(src, b, j):
        return rcopy(
            vir_ref.at[z, :, pl.ds(pl.multiple_of(xb[j] * 256, 256), 256)], v_ref[j].at[src, z],
            vy_ss.at[b, j], vy_rs.at[b, j], (block[(1, 0, 2)[b]], a),
        )

    def half(ref, e):
        return ref.at[64 * e:64 * e + 64, :]

    for j in range(2):
        for b in range(3):
            vy_copy(g, b, j).start()
    for d, p in enumerate(peers):
        meta_copy(g, d, (p, a)).start()

    def vo_copy(src, j):
        return rcopy(vir_cols(j), v_ref[j].at[src], vo_ss.at[j], vo_rs.at[j], twin)

    for j in range(2):
        vo_copy(g, j).start()

    def compute(chunk):
        def one(t, carry):
            k = chunk * CT + t
            tile_copy(k).wait()
            row = rows_s[0, k]
            occ = occ_all[lax.div(row, 4), lax.rem(row, 4)]
            for pp in range(PB // 2):
                rhs = jnp.concatenate([tile_v[k, 2 * pp], tile_v[k, 2 * pp + 1]], axis=1)
                out = jnp.dot(occ, rhs, preferred_element_type=jnp.float32)
                stage[16 * pp:16 * pp + 8, :] = out[:, :BLK]
                stage[16 * pp + 8:16 * pp + 16, :] = out[:, BLK:]
            for i in range(O):
                hbuf[i, chunk, t] = stage[pl.ds(i, PB, stride=O), :].astype(jnp.bfloat16)
            return carry

        lax.fori_loop(0, CT, one, 0)

    def h_copy(dst_g, src, chunk, d, dev):
        return rcopy(
            hbuf.at[dst_g, chunk], h_ref.at[0, chunk, src], h_ss.at[chunk, d], h_rs.at[chunk, src], dev
        )

    def h_own(chunk):
        return pltpu.make_async_copy(hbuf.at[g, chunk], h_ref.at[0, chunk, g], own_sem.at[3 + chunk])

    def hx_copy(chunk, src):
        return rcopy(
            h_ref.at[0, chunk, src], h_ref.at[1, chunk, src], hx_ss.at[chunk, src], hx_rs.at[chunk, src], mate
        )

    def mx_copy():
        return rcopy(m_ref.at[0], m_ref.at[1], mx_sem.at[0], mx_sem.at[1], mate)

    def forward_h(chunk):
        h_own(chunk).wait()
        hx_copy(chunk, g).start()
        for d, p in enumerate(peers):
            h_copy(p, p, chunk, d, (p, a)).wait_recv()
            hx_copy(chunk, p).start()

    def vz_copy(b, q, e, j):
        return rcopy(
            v_ref[j].at[block[b], quarter[q]], v_ref[j].at[block[b], quarter[q]],
            vz_ss.at[b, e, j], vz_rs.at[b, e, j], (g, x * NZ + quarter[ahead[e]]),
        )

    def zf_copy(b, q, e, j):
        rows = half(v_ref[j].at[block[b], quarter[q]], e)
        return rcopy(
            rows, rows, zf_ss.at[b, e, j], zf_rs.at[b, e, j], (g, x * NZ + quarter[ahead[e]])
        )

    def vs_copy(src, b, j):
        return rcopy(v_ref[j].at[src], v_ref[j].at[src], vs_ss.at[b, j], vs_rs.at[b, j], twin)

    def start_z(b, j):
        vy_copy(block[b], b, j).wait_recv()
        for e in range(2):
            vz_copy(b, 0, e, j).start()

    def pass_z(b, j):
        for e in range(2):
            vz_copy(b, ahead[1 - e], e, j).wait_recv()
            zf_copy(b, ahead[1 - e], e, j).start()

    def finish_z(b, j):
        for e in range(2):
            zf_copy(b, 2, e, j).wait_recv()
        vs_copy(block[b], b, j).start()

    start_z(0, 0)
    start_z(1, 0)
    for d, p in enumerate(peers):
        occ_copy(p, d, (p, a)).wait_recv()
    for chunk in range(CH):
        compute(chunk)
        for d, p in enumerate(peers):
            h_copy(p, g, chunk, d, (p, a)).start()
        h_own(chunk).start()
        if chunk == 0:
            start_z(2, 0)
            pl.semaphore_wait(ready.at[0], 1)
            pl.semaphore_signal(ready.at[1], inc=1, device_id=below, device_id_type=MESH)
        if chunk == 1:
            start_z(0, 1)
            start_z(1, 1)
        if chunk == 2:
            start_z(2, 1)
        if chunk == 3:
            m_own.wait()
            for d, p in enumerate(peers):
                meta_copy(p, d, (p, a)).wait_recv()
            mx_copy().start()
    def chain(side):
        total = m_ref[side, 0]
        for p in range(1, G):
            total += m_ref[side, p]
        key = jnp.broadcast_to(total[0:1, :], (128, 128))
        key_t = key.T
        slot = lax.broadcasted_iota(jnp.int32, (128, 128), 0)
        lane = lax.broadcasted_iota(jnp.int32, (128, 128), 1)
        before = jnp.where((key_t == key) & (slot < lane), slot + 1, 0)
        last = jnp.where(key_t == lane + 1, slot + 1, 0)
        tab_v[side, 0:1, :] = jnp.max(before, axis=0, keepdims=True)
        tab_v[side, 1:2, :] = total[1:2, :]
        tab_v[side, 2:3, :] = jnp.max(last, axis=0, keepdims=True)
        return pltpu.make_async_copy(tab_v.at[side], tab.at[side], tab_sem.at[side])

    def contract(side, j):
        def group(p, carry):
            for k in range(KMAX):
                t = p * KMAX + k
                piece = h_ref[side, k // CT, p, k % CT]
                term = jnp.dot(piece, v_ref[j][p, tab[side, 1, t]], preferred_element_type=jnp.float32)
                run[t + 1] = term + run[tab[side, 0, t]]
            return carry

        lax.fori_loop(0, G, group, 0)
        for q in range(4):
            blocks = [run[tab[side, 2, 4 * q + b]] for b in range(4)]
            done[side, j, :, q * BLK:(q + 1) * BLK] = (
                jnp.concatenate(blocks, axis=0).T.astype(jnp.bfloat16)
            )

    def columns(x_src, z_src, side):
        first = ((x_src, mate_x(x_src, c))[side] * NZ + z_src) * PDEV
        return o_ref.at[:, pl.ds(pl.multiple_of(first, PDEV), PDEV)]

    def piece_of(j, zp, side):
        return done.at[side, j, pl.ds(pl.multiple_of(zp * 64, 64), 64), :]

    def out_copy(j, d, side, x_src, z_src):
        return rcopy(
            piece_of(j, quarter[d], side), columns(x_src, z_src, side), o_ss.at[j, d, side],
            o_rs.at[j, z_src, side], (g, xb[j] * NZ + quarter[d]),
        )

    def own_copy(side):
        return pltpu.make_async_copy(piece_of(1, z, side), columns(x, z, side), o_own.at[side])

    def send_out(side, j):
        for jj, zp, d in dests:
            if jj == j:
                out_copy(j, d, side, x, z).start()
        if j == 1:
            own_copy(side).start()

    def twins(j):
        vo_copy(2 * y + 1 - c, j).wait_recv()
        v_own[j].wait()
        for b in range(3):
            vs_copy(block[b] + 1 - 2 * c, b, j).wait_recv()

    pass_z(0, 0)
    pass_z(1, 0)
    forward_h(0)
    pass_z(2, 0)
    mx_copy().wait_recv()
    tables = [chain(side) for side in range(2)]
    for cp in tables:
        cp.start()
    run[0] = jnp.zeros_like(run[0])
    finish_z(0, 0)
    finish_z(1, 0)
    forward_h(1)
    finish_z(2, 0)
    pass_z(0, 1)
    pass_z(1, 1)
    forward_h(2)
    pass_z(2, 1)
    forward_h(3)
    for cp in tables:
        cp.wait()
    twins(0)
    contract(0, 0)
    pl.semaphore_wait(ready.at[1], 1)
    send_out(0, 0)
    for b in range(3):
        finish_z(b, 1)
    twins(1)
    contract(0, 1)
    send_out(0, 1)
    for chunk in range(CH):
        for p in range(G):
            hx_copy(chunk, p).wait_recv()
    for j in range(2):
        contract(1, j)
        send_out(1, j)

    for side in range(2):
        for j, zp, d in dests:
            out_copy(j, d, side, xb[j], zp).wait_recv()
        own_copy(side).wait()
    for side in range(2):
        for j, zp, d in dests:
            out_copy(j, d, side, x, z).wait_send()

    for d, p in enumerate(peers):
        occ_copy(g, d, (p, a)).wait_send()
        meta_copy(g, d, (p, a)).wait_send()
        for chunk in range(CH):
            h_copy(p, g, chunk, d, (p, a)).wait_send()
    for j in range(2):
        for e in range(2):
            for b in range(3):
                vz_copy(b, 0, e, j).wait_send()
                zf_copy(b, ahead[1 - e], e, j).wait_send()
        for b in range(3):
            vy_copy(g, b, j).wait_send()
            vs_copy(block[b], b, j).wait_send()
    for j in range(2):
        vo_copy(g, j).wait_send()
    mx_copy().wait_send()
    for chunk in range(CH):
        for p in range(G):
            hx_copy(chunk, p).wait_send()


def whole(rows, tiles, cols, aux, count, occ, vir):
    anywhere = pl.BlockSpec(memory_space=pl.ANY)
    dma = pltpu.SemaphoreType.DMA
    return pl.pallas_call(
        whole_kernel,
        out_shape=jax.ShapeDtypeStruct((64, 16 * PDEV), jnp.bfloat16),
        in_specs=[anywhere] * 7,
        out_specs=anywhere,
        scratch_shapes=[
            pltpu.VMEM((2, CH, G, CT, PB, BLK), jnp.bfloat16),
            pltpu.VMEM((G, 4, BLK, 256), jnp.bfloat16),
            pltpu.VMEM((G, 4, BLK, 256), jnp.bfloat16),
            pltpu.VMEM((2, G, 8, 128), jnp.int32),
            pltpu.VMEM((1 + G * KMAX, PB, 256), jnp.float32),
            pltpu.VMEM((2, 2, 256, PDEV), jnp.bfloat16),
            pltpu.VMEM((2, 8, 128), jnp.int32),
            pltpu.SMEM((2, 8, 128), jnp.int32),
            pltpu.SMEM((1, KMAX), jnp.int32),
            pltpu.VMEM((1, KMAX), jnp.int32),
            pltpu.VMEM((1, KMAX), jnp.int32),
            pltpu.VMEM((1, 1), jnp.int32),
            pltpu.VMEM((O, 4 * BLK), jnp.bfloat16),
            pltpu.VMEM((KMAX, PB, BLK, BLK), jnp.bfloat16),
            pltpu.VMEM((G, 4, O, BLK), jnp.bfloat16),
            pltpu.VMEM((8, 128), jnp.int32),
            pltpu.VMEM((PB * O, BLK), jnp.float32),
            pltpu.VMEM((O, CH, CT, PB, BLK), jnp.bfloat16),
            dma((5,)), dma((KMAX,)), dma((3 + CH,)),
            dma((7,)), dma((G,)), dma((7,)), dma((G,)), dma((2,)),
            dma((CH, 7)), dma((CH, G)), dma((CH, G)), dma((CH, G)),
            dma((3, 2)), dma((3, 2)),
            dma((3, 2, 2)), dma((3, 2, 2)), dma((3, 2, 2)), dma((3, 2, 2)),
            dma((2,)), dma((2,)), dma((3, 2)), dma((3, 2)),
            dma((2,)), dma((2,)), dma((2, NZ, 2)), dma((2, NZ, 2)),
            pltpu.SemaphoreType.REGULAR((2,)),
        ],
        compiler_params=pltpu.CompilerParams(
            collective_id=0, has_side_effects=True, vmem_limit_bytes=60 * 1024 * 1024
        ),
        name="whole",
    )(rows, tiles, cols, aux, count, occ, vir)


def shards(integral_tiles, row_blocks, col_blocks, aux_blocks, tile_counts, occ_coeffs, vir_coeffs):
    result = whole(
        row_blocks.reshape(1, KMAX),
        integral_tiles.reshape(KMAX, PB, BLK, BLK),
        col_blocks.reshape(1, KMAX),
        aux_blocks.reshape(1, KMAX),
        tile_counts,
        occ_coeffs,
        vir_coeffs.reshape(4, BLK, V),
    )
    return result.astype(jnp.float32)


def solution(mesh):
    in_specs = (
        P("grp", "aux", None, None, None, None),
        P("grp", "aux", None),
        P("grp", "aux", None),
        P("grp", "aux", None),
        P("grp", "aux"),
        P(None, "grp"),
        P("grp", None),
    )
    out_specs = P(("grp", "aux"), None)
    return jax.shard_map(shards, mesh=mesh, in_specs=in_specs, out_specs=out_specs, check_vma=False)
```

```python
import functools

import jax
import jax.numpy as jnp
from jax import lax
from jax.experimental import pallas as pl
from jax.experimental.pallas import tpu as pltpu
from jax.sharding import PartitionSpec as P

O = 8
V = 1024
BLK = 128
PB = 32
PDEV = 512
KMAX = 12
G = 8
NZ = 4
CH = 4
CT = KMAX // CH
MESH = pl.DeviceIdType.MESH


def rcopy(src, dst, ssem, rsem, dev):
    return pltpu.make_async_remote_copy(
        src_ref=src, dst_ref=dst, send_sem=ssem, recv_sem=rsem, device_id=dev, device_id_type=MESH
    )


def where_am_i():
    g = lax.axis_index("grp")
    a = lax.axis_index("aux")
    return g, a, lax.div(g, 2), lax.rem(g, 2), lax.div(a, NZ), lax.rem(a, NZ)


def mate_x(x, c):
    odd = lax.rem(x, 2)
    return lax.rem(x + 4 + (1 - 2 * odd) * (1 - 2 * c), 4)


def whole_kernel(
    rows_ref, tiles_ref, cols_ref, aux_ref, count_ref, occ_ref, vir_ref,
    o_ref,
    h_ref, vf_ref, vn_ref, m_ref, run, done, tab_v, tab,
    rows_s, cols_v, aux_v, count_v, occ_v, tile_v, occ_all, meta_own, stage, hbuf,
    in_sem, tile_sem, own_sem,
    occ_ss, occ_rs, meta_ss, meta_rs, mx_sem,
    h_ss, h_rs, hx_ss, hx_rs,
    vy_ss, vy_rs, vz_ss, vz_rs, zf_ss, zf_rs, vo_ss, vo_rs, vs_ss, vs_rs,
    tab_sem, o_own, o_ss, o_rs, ready,
):
    g, a, y, c, x, z = where_am_i()
    xm = mate_x(x, c)
    mate = (g, xm * NZ + z)
    twin = (2 * y + 1 - c, a)
    xb = (lax.rem(x + 2, 4), x)
    v_ref = (vf_ref, vn_ref)

    small = [
        pltpu.make_async_copy(src, dst, in_sem.at[n])
        for n, (src, dst) in enumerate((
            (occ_ref, occ_v), (cols_ref, cols_v), (aux_ref, aux_v), (count_ref, count_v), (rows_ref, rows_s)
        ))
    ]
    for cp in small:
        cp.start()

    peers = [2 * lax.rem(y + d, 4) + lax.rem(c + e, 2) for d, e in ((0, 1), (1, 0), (3, 0), (1, 1), (3, 1), (2, 0), (2, 1))]
    around = [2 * lax.rem(y + d, 4) + c for d in range(4)]
    quarter = [lax.rem(z + d, NZ) for d in range(4)]
    block = (around[3], around[1], around[2])
    ahead = (1, 3)
    dests = [(j, quarter[d], d) for j in range(2) for d in (2, 1, 3, 0) if (d, j) != (0, 1)]

    barrier = pltpu.get_barrier_semaphore()
    for p in peers:
        pl.semaphore_signal(barrier, inc=1, device_id=(p, a), device_id_type=MESH)
    below = (g, lax.rem(x + 3, 4) * NZ + z)
    above = (g, lax.rem(x + 1, 4) * NZ + z)
    for dev in (below, above):
        pl.semaphore_signal(barrier, inc=1, device_id=dev, device_id_type=MESH)
    for zp in quarter[1:]:
        pl.semaphore_signal(barrier, inc=1, device_id=(g, x * NZ + zp), device_id_type=MESH)

    def tile_copy(k):
        return pltpu.make_async_copy(tiles_ref.at[k], tile_v.at[k], tile_sem.at[k])

    for k in range(KMAX):
        tile_copy(k).start()

    def vir_cols(j):
        return vir_ref.at[:, :, pl.ds(pl.multiple_of(xb[j] * 256, 256), 256)]

    v_own = [pltpu.make_async_copy(vir_cols(j), v_ref[j].at[g], own_sem.at[j]) for j in range(2)]
    for cp in v_own:
        cp.start()

    small[0].wait()
    for b in range(4):
        occ_all[g, b] = occ_v[:, b * BLK:(b + 1) * BLK]
    pl.semaphore_wait(barrier, 12)
    pl.semaphore_signal(ready.at[0], inc=1, device_id=below, device_id_type=MESH)

    def occ_copy(src, d, dev):
        return rcopy(occ_all.at[src], occ_all.at[src], occ_ss.at[d], occ_rs.at[src], dev)

    def meta_copy(src, d, dev):
        return rcopy(meta_own, m_ref.at[0, src], meta_ss.at[d], meta_rs.at[src], dev)

    for d, p in enumerate(peers):
        occ_copy(g, d, (p, a)).start()

    def vy_copy(src, b, j):
        return rcopy(
            vir_ref.at[z, :, pl.ds(pl.multiple_of(xb[j] * 256, 256), 256)], v_ref[j].at[src, z],
            vy_ss.at[b, j], vy_rs.at[b, j], (block[(1, 0, 2)[b]], a),
        )

    def half(ref, e):
        return ref.at[64 * e:64 * e + 64, :]

    for j in range(2):
        for b in range(3):
            vy_copy(g, b, j).start()
    for cp in small[1:]:
        cp.wait()
    meta_own[...] = jnp.zeros_like(meta_own)
    kept = lax.broadcasted_iota(jnp.int32, (1, KMAX), 1) < count_v[...]
    meta_own[0:1, 0:KMAX] = jnp.where(kept, aux_v[...] + 1, 0)
    meta_own[1:2, 0:KMAX] = cols_v[...]
    meta_own[...] = pltpu.roll(meta_own[...], KMAX * g, 1)
    m_own = pltpu.make_async_copy(meta_own, m_ref.at[0, g], own_sem.at[2])
    m_own.start()
    for d, p in enumerate(peers):
        meta_copy(g, d, (p, a)).start()

    def vo_copy(src, j):
        return rcopy(vir_cols(j), v_ref[j].at[src], vo_ss.at[j], vo_rs.at[j], twin)

    for j in range(2):
        vo_copy(g, j).start()

    def compute(chunk):
        def one(t, carry):
            k = chunk * CT + t
            tile_copy(k).wait()
            row = rows_s[0, k]
            occ = occ_all[lax.div(row, 4), lax.rem(row, 4)]
            for pp in range(PB // 2):
                rhs = jnp.concatenate([tile_v[k, 2 * pp], tile_v[k, 2 * pp + 1]], axis=1)
                out = jnp.dot(occ, rhs, preferred_element_type=jnp.float32)
                stage[16 * pp:16 * pp + 8, :] = out[:, :BLK]
                stage[16 * pp + 8:16 * pp + 16, :] = out[:, BLK:]
            for i in range(O):
                hbuf[i, chunk, t] = stage[pl.ds(i, PB, stride=O), :].astype(jnp.bfloat16)
            return carry

        lax.fori_loop(0, CT, one, 0)

    def h_copy(dst_g, src, chunk, d, dev):
        return rcopy(
            hbuf.at[dst_g, chunk], h_ref.at[0, chunk, src], h_ss.at[chunk, d], h_rs.at[chunk, src], dev
        )

    def h_own(chunk):
        return pltpu.make_async_copy(hbuf.at[g, chunk], h_ref.at[0, chunk, g], own_sem.at[3 + chunk])

    def hx_copy(chunk, src):
        return rcopy(
            h_ref.at[0, chunk, src], h_ref.at[1, chunk, src], hx_ss.at[chunk, src], hx_rs.at[chunk, src], mate
        )

    def mx_copy():
        return rcopy(m_ref.at[0], m_ref.at[1], mx_sem.at[0], mx_sem.at[1], mate)

    def forward_h(chunk):
        h_own(chunk).wait()
        hx_copy(chunk, g).start()
        for d, p in enumerate(peers):
            h_copy(p, p, chunk, d, (p, a)).wait_recv()
            hx_copy(chunk, p).start()

    def vz_copy(b, q, e, j):
        return rcopy(
            v_ref[j].at[block[b], quarter[q]], v_ref[j].at[block[b], quarter[q]],
            vz_ss.at[b, e, j], vz_rs.at[b, e, j], (g, x * NZ + quarter[ahead[e]]),
        )

    def zf_copy(b, q, e, j):
        rows = half(v_ref[j].at[block[b], quarter[q]], e)
        return rcopy(
            rows, rows, zf_ss.at[b, e, j], zf_rs.at[b, e, j], (g, x * NZ + quarter[ahead[e]])
        )

    def vs_copy(src, b, j):
        return rcopy(v_ref[j].at[src], v_ref[j].at[src], vs_ss.at[b, j], vs_rs.at[b, j], twin)

    def start_z(b, j):
        vy_copy(block[b], b, j).wait_recv()
        for e in range(2):
            vz_copy(b, 0, e, j).start()

    def pass_z(b, j):
        for e in range(2):
            vz_copy(b, ahead[1 - e], e, j).wait_recv()
            zf_copy(b, ahead[1 - e], e, j).start()

    def finish_z(b, j):
        for e in range(2):
            zf_copy(b, 2, e, j).wait_recv()
        vs_copy(block[b], b, j).start()

    start_z(0, 0)
    start_z(1, 0)
    for d, p in enumerate(peers):
        occ_copy(p, d, (p, a)).wait_recv()
    for chunk in range(CH):
        compute(chunk)
        for d, p in enumerate(peers):
            h_copy(p, g, chunk, d, (p, a)).start()
        h_own(chunk).start()
        if chunk == 0:
            start_z(2, 0)
            pl.semaphore_wait(ready.at[0], 1)
            pl.semaphore_signal(ready.at[1], inc=1, device_id=below, device_id_type=MESH)
        if chunk == 1:
            start_z(0, 1)
            start_z(1, 1)
        if chunk == 2:
            start_z(2, 1)
        if chunk == 3:
            m_own.wait()
            for d, p in enumerate(peers):
                meta_copy(p, d, (p, a)).wait_recv()
            mx_copy().start()
    def chain(side):
        total = m_ref[side, 0]
        for p in range(1, G):
            total += m_ref[side, p]
        key = jnp.broadcast_to(total[0:1, :], (128, 128))
        key_t = key.T
        slot = lax.broadcasted_iota(jnp.int32, (128, 128), 0)
        lane = lax.broadcasted_iota(jnp.int32, (128, 128), 1)
        before = jnp.where((key_t == key) & (slot < lane), slot + 1, 0)
        last = jnp.where(key_t == lane + 1, slot + 1, 0)
        tab_v[side, 0:1, :] = jnp.max(before, axis=0, keepdims=True)
        tab_v[side, 1:2, :] = total[1:2, :]
        tab_v[side, 2:3, :] = jnp.max(last, axis=0, keepdims=True)
        return pltpu.make_async_copy(tab_v.at[side], tab.at[side], tab_sem.at[side])

    def contract(side, j):
        def group(step, carry):
            for n in range(2 * KMAX):
                k = n % KMAX
                p = 2 * step + n // KMAX
                t = 2 * KMAX * step + n
                piece = h_ref[side, k // CT, p, k % CT]
                term = jnp.dot(piece, v_ref[j][p, tab[side, 1, t]], preferred_element_type=jnp.float32)
                run[t + 1] = term + run[tab[side, 0, t]]
            return carry

        lax.fori_loop(0, G // 2, group, 0)
        for q in range(4):
            blocks = [run[tab[side, 2, 4 * q + b]] for b in range(4)]
            done[side, j, :, q * BLK:(q + 1) * BLK] = (
                jnp.concatenate(blocks, axis=0).T.astype(jnp.bfloat16)
            )

    def columns(x_src, z_src, side):
        first = ((x_src, mate_x(x_src, c))[side] * NZ + z_src) * PDEV
        return o_ref.at[:, pl.ds(pl.multiple_of(first, PDEV), PDEV)]

    def piece_of(j, zp, side):
        return done.at[side, j, pl.ds(pl.multiple_of(zp * 64, 64), 64), :]

    def out_copy(j, d, side, x_src, z_src):
        return rcopy(
            piece_of(j, quarter[d], side), columns(x_src, z_src, side), o_ss.at[j, d, side],
            o_rs.at[j, z_src, side], (g, xb[j] * NZ + quarter[d]),
        )

    def own_copy(side):
        return pltpu.make_async_copy(piece_of(1, z, side), columns(x, z, side), o_own.at[side])

    def send_out(side, j):
        for jj, zp, d in dests:
            if jj == j:
                out_copy(j, d, side, x, z).start()
        if j == 1:
            own_copy(side).start()

    def twins(j):
        vo_copy(2 * y + 1 - c, j).wait_recv()
        v_own[j].wait()
        for b in range(3):
            vs_copy(block[b] + 1 - 2 * c, b, j).wait_recv()

    pass_z(0, 0)
    pass_z(1, 0)
    forward_h(0)
    pass_z(2, 0)
    mx_copy().wait_recv()
    tables = [chain(side) for side in range(2)]
    for cp in tables:
        cp.start()
    run[0] = jnp.zeros_like(run[0])
    finish_z(0, 0)
    finish_z(1, 0)
    forward_h(1)
    finish_z(2, 0)
    pass_z(0, 1)
    pass_z(1, 1)
    forward_h(2)
    pass_z(2, 1)
    forward_h(3)
    for cp in tables:
        cp.wait()
    twins(0)
    contract(0, 0)
    pl.semaphore_wait(ready.at[1], 1)
    send_out(0, 0)
    for b in range(3):
        finish_z(b, 1)
    twins(1)
    contract(0, 1)
    send_out(0, 1)
    for chunk in range(CH):
        for p in range(G):
            hx_copy(chunk, p).wait_recv()
    for j in range(2):
        contract(1, j)
        send_out(1, j)

    for side in range(2):
        for j, zp, d in dests:
            out_copy(j, d, side, xb[j], zp).wait_recv()
        own_copy(side).wait()
    for side in range(2):
        for j, zp, d in dests:
            out_copy(j, d, side, x, z).wait_send()

    for d, p in enumerate(peers):
        occ_copy(g, d, (p, a)).wait_send()
        meta_copy(g, d, (p, a)).wait_send()
        for chunk in range(CH):
            h_copy(p, g, chunk, d, (p, a)).wait_send()
    for j in range(2):
        for e in range(2):
            for b in range(3):
                vz_copy(b, 0, e, j).wait_send()
                zf_copy(b, ahead[1 - e], e, j).wait_send()
        for b in range(3):
            vy_copy(g, b, j).wait_send()
            vs_copy(block[b], b, j).wait_send()
    for j in range(2):
        vo_copy(g, j).wait_send()
    mx_copy().wait_send()
    for chunk in range(CH):
        for p in range(G):
            hx_copy(chunk, p).wait_send()


def whole(rows, tiles, cols, aux, count, occ, vir):
    anywhere = pl.BlockSpec(memory_space=pl.ANY)
    dma = pltpu.SemaphoreType.DMA
    return pl.pallas_call(
        whole_kernel,
        out_shape=jax.ShapeDtypeStruct((64, 16 * PDEV), jnp.bfloat16),
        in_specs=[anywhere] * 7,
        out_specs=anywhere,
        scratch_shapes=[
            pltpu.VMEM((2, CH, G, CT, PB, BLK), jnp.bfloat16),
            pltpu.VMEM((G, 4, BLK, 256), jnp.bfloat16),
            pltpu.VMEM((G, 4, BLK, 256), jnp.bfloat16),
            pltpu.VMEM((2, G, 8, 128), jnp.int32),
            pltpu.VMEM((1 + G * KMAX, PB, 256), jnp.float32),
            pltpu.VMEM((2, 2, 256, PDEV), jnp.bfloat16),
            pltpu.VMEM((2, 8, 128), jnp.int32),
            pltpu.SMEM((2, 8, 128), jnp.int32),
            pltpu.SMEM((1, KMAX), jnp.int32),
            pltpu.VMEM((1, KMAX), jnp.int32),
            pltpu.VMEM((1, KMAX), jnp.int32),
            pltpu.VMEM((1, 1), jnp.int32),
            pltpu.VMEM((O, 4 * BLK), jnp.bfloat16),
            pltpu.VMEM((KMAX, PB, BLK, BLK), jnp.bfloat16),
            pltpu.VMEM((G, 4, O, BLK), jnp.bfloat16),
            pltpu.VMEM((8, 128), jnp.int32),
            pltpu.VMEM((PB * O, BLK), jnp.float32),
            pltpu.VMEM((O, CH, CT, PB, BLK), jnp.bfloat16),
            dma((5,)), dma((KMAX,)), dma((3 + CH,)),
            dma((7,)), dma((G,)), dma((7,)), dma((G,)), dma((2,)),
            dma((CH, 7)), dma((CH, G)), dma((CH, G)), dma((CH, G)),
            dma((3, 2)), dma((3, 2)),
            dma((3, 2, 2)), dma((3, 2, 2)), dma((3, 2, 2)), dma((3, 2, 2)),
            dma((2,)), dma((2,)), dma((3, 2)), dma((3, 2)),
            dma((2,)), dma((2,)), dma((2, NZ, 2)), dma((2, NZ, 2)),
            pltpu.SemaphoreType.REGULAR((2,)),
        ],
        compiler_params=pltpu.CompilerParams(
            collective_id=0, has_side_effects=True, vmem_limit_bytes=60 * 1024 * 1024
        ),
        name="whole",
    )(rows, tiles, cols, aux, count, occ, vir)


def widen_kernel(src, dst, narrow, wide, in_sem, out_sem):
    pieces = 8
    width = 16 * PDEV // pieces

    def columns(ref, n):
        return ref.at[:, n * width:(n + 1) * width]

    loads = [pltpu.make_async_copy(columns(src, n), narrow.at[n], in_sem.at[n]) for n in range(pieces)]
    stores = [pltpu.make_async_copy(wide.at[n], columns(dst, n), out_sem.at[n]) for n in range(pieces)]
    for cp in loads:
        cp.start()
    for n in range(pieces):
        loads[n].wait()
        wide[n] = narrow[n].astype(jnp.float32)
        stores[n].start()
    for cp in stores:
        cp.wait()


def widen(result):
    anywhere = pl.BlockSpec(memory_space=pl.ANY)
    return pl.pallas_call(
        widen_kernel,
        out_shape=jax.ShapeDtypeStruct((64, 16 * PDEV), jnp.float32),
        in_specs=[anywhere],
        out_specs=anywhere,
        scratch_shapes=[
            pltpu.VMEM((8, 64, 2 * PDEV), jnp.bfloat16),
            pltpu.VMEM((8, 64, 2 * PDEV), jnp.float32),
            pltpu.SemaphoreType.DMA((8,)),
            pltpu.SemaphoreType.DMA((8,)),
        ],
        name="widen",
    )(result)


def shards(integral_tiles, row_blocks, col_blocks, aux_blocks, tile_counts, occ_coeffs, vir_coeffs):
    result = whole(
        row_blocks.reshape(1, KMAX),
        integral_tiles.reshape(KMAX, PB, BLK, BLK),
        col_blocks.reshape(1, KMAX),
        aux_blocks.reshape(1, KMAX),
        tile_counts,
        occ_coeffs,
        vir_coeffs.reshape(4, BLK, V),
    )
    return widen(result)


def solution(mesh):
    in_specs = (
        P("grp", "aux", None, None, None, None),
        P("grp", "aux", None),
        P("grp", "aux", None),
        P("grp", "aux", None),
        P("grp", "aux"),
        P(None, "grp"),
        P("grp", None),
    )
    out_specs = P(("grp", "aux"), None)
    return jax.shard_map(shards, mesh=mesh, in_specs=in_specs, out_specs=out_specs, check_vma=False)
```

```python
import functools

import jax
import jax.numpy as jnp
from jax import lax
from jax.experimental import pallas as pl
from jax.experimental.pallas import tpu as pltpu
from jax.sharding import PartitionSpec as P

O = 8
V = 1024
BLK = 128
PB = 32
PDEV = 512
KMAX = 12
G = 8
NZ = 4
CH = 3
CT = KMAX // CH
MESH = pl.DeviceIdType.MESH


def rcopy(src, dst, ssem, rsem, dev):
    return pltpu.make_async_remote_copy(
        src_ref=src, dst_ref=dst, send_sem=ssem, recv_sem=rsem, device_id=dev, device_id_type=MESH
    )


def where_am_i():
    g = lax.axis_index("grp")
    a = lax.axis_index("aux")
    return g, a, lax.div(g, 2), lax.rem(g, 2), lax.div(a, NZ), lax.rem(a, NZ)


def mate_x(x, c):
    odd = lax.rem(x, 2)
    return lax.rem(x + 4 + (1 - 2 * odd) * (1 - 2 * c), 4)


def whole_kernel(
    rows_ref, tiles_ref, cols_ref, aux_ref, count_ref, occ_ref, vir_ref,
    o_ref,
    h_ref, vf_ref, vn_ref, m_ref, run, done, tab_v, tab,
    rows_s, cols_v, aux_v, count_v, occ_v, tile_v, occ_all, meta_own, stage, hbuf,
    in_sem, tile_sem, own_sem,
    occ_ss, occ_rs, meta_ss, meta_rs, mx_sem,
    h_ss, h_rs, hx_ss, hx_rs,
    vy_ss, vy_rs, vz_ss, vz_rs, zf_ss, zf_rs, vo_ss, vo_rs, vs_ss, vs_rs,
    tab_sem, o_own, o_ss, o_rs, ready,
):
    g, a, y, c, x, z = where_am_i()
    xm = mate_x(x, c)
    mate = (g, xm * NZ + z)
    twin = (2 * y + 1 - c, a)
    xb = (lax.rem(x + 2, 4), x)
    v_ref = (vf_ref, vn_ref)

    small = [
        pltpu.make_async_copy(src, dst, in_sem.at[n])
        for n, (src, dst) in enumerate((
            (occ_ref, occ_v), (cols_ref, cols_v), (aux_ref, aux_v), (count_ref, count_v), (rows_ref, rows_s)
        ))
    ]
    for cp in small:
        cp.start()

    peers = [2 * lax.rem(y + d, 4) + lax.rem(c + e, 2) for d, e in ((0, 1), (1, 0), (3, 0), (1, 1), (3, 1), (2, 0), (2, 1))]
    around = [2 * lax.rem(y + d, 4) + c for d in range(4)]
    quarter = [lax.rem(z + d, NZ) for d in range(4)]
    block = (around[3], around[1], around[2])
    ahead = (1, 3)
    dests = [(j, quarter[d], d) for j in range(2) for d in (2, 1, 3, 0) if (d, j) != (0, 1)]

    barrier = pltpu.get_barrier_semaphore()
    for p in peers:
        pl.semaphore_signal(barrier, inc=1, device_id=(p, a), device_id_type=MESH)
    below = (g, lax.rem(x + 3, 4) * NZ + z)
    above = (g, lax.rem(x + 1, 4) * NZ + z)
    for dev in (below, above):
        pl.semaphore_signal(barrier, inc=1, device_id=dev, device_id_type=MESH)
    for zp in quarter[1:]:
        pl.semaphore_signal(barrier, inc=1, device_id=(g, x * NZ + zp), device_id_type=MESH)

    def tile_copy(k):
        return pltpu.make_async_copy(tiles_ref.at[k], tile_v.at[k], tile_sem.at[k])

    for k in range(KMAX):
        tile_copy(k).start()

    def vir_cols(j):
        return vir_ref.at[:, :, pl.ds(pl.multiple_of(xb[j] * 256, 256), 256)]

    v_own = [pltpu.make_async_copy(vir_cols(j), v_ref[j].at[g], own_sem.at[j]) for j in range(2)]
    for cp in v_own:
        cp.start()

    small[0].wait()
    for b in range(4):
        occ_all[g, b] = occ_v[:, b * BLK:(b + 1) * BLK]
    pl.semaphore_wait(barrier, 12)
    pl.semaphore_signal(ready.at[0], inc=1, device_id=below, device_id_type=MESH)

    def occ_copy(src, d, dev):
        return rcopy(occ_all.at[src], occ_all.at[src], occ_ss.at[d], occ_rs.at[src], dev)

    def meta_copy(src, d, dev):
        return rcopy(meta_own, m_ref.at[0, src], meta_ss.at[d], meta_rs.at[src], dev)

    for d, p in enumerate(peers):
        occ_copy(g, d, (p, a)).start()

    def vy_copy(src, b, j):
        return rcopy(
            vir_ref.at[z, :, pl.ds(pl.multiple_of(xb[j] * 256, 256), 256)], v_ref[j].at[src, z],
            vy_ss.at[b, j], vy_rs.at[b, j], (block[(1, 0, 2)[b]], a),
        )

    def half(ref, e):
        return ref.at[64 * e:64 * e + 64, :]

    for j in range(2):
        for b in range(3):
            vy_copy(g, b, j).start()
    for cp in small[1:]:
        cp.wait()
    meta_own[...] = jnp.zeros_like(meta_own)
    kept = lax.broadcasted_iota(jnp.int32, (1, KMAX), 1) < count_v[...]
    meta_own[0:1, 0:KMAX] = jnp.where(kept, aux_v[...] + 1, 0)
    meta_own[1:2, 0:KMAX] = cols_v[...]
    meta_own[...] = pltpu.roll(meta_own[...], KMAX * g, 1)
    m_own = pltpu.make_async_copy(meta_own, m_ref.at[0, g], own_sem.at[2])
    m_own.start()
    for d, p in enumerate(peers):
        meta_copy(g, d, (p, a)).start()

    def vo_copy(src, j):
        return rcopy(vir_cols(j), v_ref[j].at[src], vo_ss.at[j], vo_rs.at[j], twin)

    for j in range(2):
        vo_copy(g, j).start()

    def compute(chunk):
        def one(t, carry):
            k = chunk * CT + t
            tile_copy(k).wait()
            row = rows_s[0, k]
            occ = occ_all[lax.div(row, 4), lax.rem(row, 4)]
            for pp in range(PB // 2):
                rhs = jnp.concatenate([tile_v[k, 2 * pp], tile_v[k, 2 * pp + 1]], axis=1)
                out = jnp.dot(occ, rhs, preferred_element_type=jnp.float32)
                stage[16 * pp:16 * pp + 8, :] = out[:, :BLK]
                stage[16 * pp + 8:16 * pp + 16, :] = out[:, BLK:]
            for i in range(O):
                hbuf[i, chunk, t] = stage[pl.ds(i, PB, stride=O), :].astype(jnp.bfloat16)
            return carry

        lax.fori_loop(0, CT, one, 0)

    def h_copy(dst_g, src, chunk, d, dev):
        return rcopy(
            hbuf.at[dst_g, chunk], h_ref.at[0, chunk, src], h_ss.at[chunk, d], h_rs.at[chunk, src], dev
        )

    def h_own(chunk):
        return pltpu.make_async_copy(hbuf.at[g, chunk], h_ref.at[0, chunk, g], own_sem.at[3 + chunk])

    def hx_copy(chunk, src):
        return rcopy(
            h_ref.at[0, chunk, src], h_ref.at[1, chunk, src], hx_ss.at[chunk, src], hx_rs.at[chunk, src], mate
        )

    def mx_copy():
        return rcopy(m_ref.at[0], m_ref.at[1], mx_sem.at[0], mx_sem.at[1], mate)

    def forward_h(chunk):
        h_own(chunk).wait()
        hx_copy(chunk, g).start()
        for d, p in enumerate(peers):
            h_copy(p, p, chunk, d, (p, a)).wait_recv()
            hx_copy(chunk, p).start()

    def vz_copy(b, q, e, j):
        return rcopy(
            v_ref[j].at[block[b], quarter[q]], v_ref[j].at[block[b], quarter[q]],
            vz_ss.at[b, e, j], vz_rs.at[b, e, j], (g, x * NZ + quarter[ahead[e]]),
        )

    def zf_copy(b, q, e, j):
        rows = half(v_ref[j].at[block[b], quarter[q]], e)
        return rcopy(
            rows, rows, zf_ss.at[b, e, j], zf_rs.at[b, e, j], (g, x * NZ + quarter[ahead[e]])
        )

    def vs_copy(src, b, j):
        return rcopy(v_ref[j].at[src], v_ref[j].at[src], vs_ss.at[b, j], vs_rs.at[b, j], twin)

    def start_z(b, j):
        vy_copy(block[b], b, j).wait_recv()
        for e in range(2):
            vz_copy(b, 0, e, j).start()

    def pass_z(b, j):
        for e in range(2):
            vz_copy(b, ahead[1 - e], e, j).wait_recv()
            zf_copy(b, ahead[1 - e], e, j).start()

    def finish_z(b, j):
        for e in range(2):
            zf_copy(b, 2, e, j).wait_recv()
        vs_copy(block[b], b, j).start()

    start_z(0, 0)
    start_z(1, 0)
    for d, p in enumerate(peers):
        occ_copy(p, d, (p, a)).wait_recv()
    for chunk in range(CH):
        compute(chunk)
        for d, p in enumerate(peers):
            h_copy(p, g, chunk, d, (p, a)).start()
        h_own(chunk).start()
        if chunk == 0:
            start_z(2, 0)
            pl.semaphore_wait(ready.at[0], 1)
            pl.semaphore_signal(ready.at[1], inc=1, device_id=below, device_id_type=MESH)
        if chunk == 1:
            start_z(0, 1)
            start_z(1, 1)
        if chunk == 2:
            start_z(2, 1)
        if chunk == 2:
            m_own.wait()
            for d, p in enumerate(peers):
                meta_copy(p, d, (p, a)).wait_recv()
            mx_copy().start()
    def chain(side):
        total = m_ref[side, 0]
        for p in range(1, G):
            total += m_ref[side, p]
        key = jnp.broadcast_to(total[0:1, :], (128, 128))
        key_t = key.T
        slot = lax.broadcasted_iota(jnp.int32, (128, 128), 0)
        lane = lax.broadcasted_iota(jnp.int32, (128, 128), 1)
        before = jnp.where((key_t == key) & (slot < lane), slot + 1, 0)
        last = jnp.where(key_t == lane + 1, slot + 1, 0)
        tab_v[side, 0:1, :] = jnp.max(before, axis=0, keepdims=True)
        tab_v[side, 1:2, :] = total[1:2, :]
        tab_v[side, 2:3, :] = jnp.max(last, axis=0, keepdims=True)
        return pltpu.make_async_copy(tab_v.at[side], tab.at[side], tab_sem.at[side])

    def contract(side, j):
        def group(step, carry):
            for n in range(2 * KMAX):
                k = n % KMAX
                p = 2 * step + n // KMAX
                t = 2 * KMAX * step + n
                piece = h_ref[side, k // CT, p, k % CT]
                term = jnp.dot(piece, v_ref[j][p, tab[side, 1, t]], preferred_element_type=jnp.float32)
                run[t + 1] = term + run[tab[side, 0, t]]
            return carry

        lax.fori_loop(0, G // 2, group, 0)
        for q in range(4):
            blocks = [run[tab[side, 2, 4 * q + b]] for b in range(4)]
            done[side, j, :, q * BLK:(q + 1) * BLK] = (
                jnp.concatenate(blocks, axis=0).T.astype(jnp.bfloat16)
            )

    def columns(x_src, z_src, side):
        first = ((x_src, mate_x(x_src, c))[side] * NZ + z_src) * PDEV
        return o_ref.at[:, pl.ds(pl.multiple_of(first, PDEV), PDEV)]

    def piece_of(j, zp, side):
        return done.at[side, j, pl.ds(pl.multiple_of(zp * 64, 64), 64), :]

    def out_copy(j, d, side, x_src, z_src):
        return rcopy(
            piece_of(j, quarter[d], side), columns(x_src, z_src, side), o_ss.at[j, d, side],
            o_rs.at[j, z_src, side], (g, xb[j] * NZ + quarter[d]),
        )

    def own_copy(side):
        return pltpu.make_async_copy(piece_of(1, z, side), columns(x, z, side), o_own.at[side])

    def send_out(side, j):
        for jj, zp, d in dests:
            if jj == j:
                out_copy(j, d, side, x, z).start()
        if j == 1:
            own_copy(side).start()

    def twins(j):
        vo_copy(2 * y + 1 - c, j).wait_recv()
        v_own[j].wait()
        for b in range(3):
            vs_copy(block[b] + 1 - 2 * c, b, j).wait_recv()

    pass_z(0, 0)
    pass_z(1, 0)
    forward_h(0)
    pass_z(2, 0)
    mx_copy().wait_recv()
    tables = [chain(side) for side in range(2)]
    for cp in tables:
        cp.start()
    run[0] = jnp.zeros_like(run[0])
    finish_z(0, 0)
    finish_z(1, 0)
    forward_h(1)
    finish_z(2, 0)
    pass_z(0, 1)
    pass_z(1, 1)
    pass_z(2, 1)
    forward_h(2)
    for cp in tables:
        cp.wait()
    twins(0)
    contract(0, 0)
    pl.semaphore_wait(ready.at[1], 1)
    send_out(0, 0)
    for b in range(3):
        finish_z(b, 1)
    twins(1)
    contract(0, 1)
    send_out(0, 1)
    for chunk in range(CH):
        for p in range(G):
            hx_copy(chunk, p).wait_recv()
    for j in range(2):
        contract(1, j)
        send_out(1, j)

    for side in range(2):
        for j, zp, d in dests:
            out_copy(j, d, side, xb[j], zp).wait_recv()
        own_copy(side).wait()
    for side in range(2):
        for j, zp, d in dests:
            out_copy(j, d, side, x, z).wait_send()

    for d, p in enumerate(peers):
        occ_copy(g, d, (p, a)).wait_send()
        meta_copy(g, d, (p, a)).wait_send()
        for chunk in range(CH):
            h_copy(p, g, chunk, d, (p, a)).wait_send()
    for j in range(2):
        for e in range(2):
            for b in range(3):
                vz_copy(b, 0, e, j).wait_send()
                zf_copy(b, ahead[1 - e], e, j).wait_send()
        for b in range(3):
            vy_copy(g, b, j).wait_send()
            vs_copy(block[b], b, j).wait_send()
    for j in range(2):
        vo_copy(g, j).wait_send()
    mx_copy().wait_send()
    for chunk in range(CH):
        for p in range(G):
            hx_copy(chunk, p).wait_send()


def whole(rows, tiles, cols, aux, count, occ, vir):
    anywhere = pl.BlockSpec(memory_space=pl.ANY)
    dma = pltpu.SemaphoreType.DMA
    return pl.pallas_call(
        whole_kernel,
        out_shape=jax.ShapeDtypeStruct((64, 16 * PDEV), jnp.bfloat16),
        in_specs=[anywhere] * 7,
        out_specs=anywhere,
        scratch_shapes=[
            pltpu.VMEM((2, CH, G, CT, PB, BLK), jnp.bfloat16),
            pltpu.VMEM((G, 4, BLK, 256), jnp.bfloat16),
            pltpu.VMEM((G, 4, BLK, 256), jnp.bfloat16),
            pltpu.VMEM((2, G, 8, 128), jnp.int32),
            pltpu.VMEM((1 + G * KMAX, PB, 256), jnp.float32),
            pltpu.VMEM((2, 2, 256, PDEV), jnp.bfloat16),
            pltpu.VMEM((2, 8, 128), jnp.int32),
            pltpu.SMEM((2, 8, 128), jnp.int32),
            pltpu.SMEM((1, KMAX), jnp.int32),
            pltpu.VMEM((1, KMAX), jnp.int32),
            pltpu.VMEM((1, KMAX), jnp.int32),
            pltpu.VMEM((1, 1), jnp.int32),
            pltpu.VMEM((O, 4 * BLK), jnp.bfloat16),
            pltpu.VMEM((KMAX, PB, BLK, BLK), jnp.bfloat16),
            pltpu.VMEM((G, 4, O, BLK), jnp.bfloat16),
            pltpu.VMEM((8, 128), jnp.int32),
            pltpu.VMEM((PB * O, BLK), jnp.float32),
            pltpu.VMEM((O, CH, CT, PB, BLK), jnp.bfloat16),
            dma((5,)), dma((KMAX,)), dma((3 + CH,)),
            dma((7,)), dma((G,)), dma((7,)), dma((G,)), dma((2,)),
            dma((CH, 7)), dma((CH, G)), dma((CH, G)), dma((CH, G)),
            dma((3, 2)), dma((3, 2)),
            dma((3, 2, 2)), dma((3, 2, 2)), dma((3, 2, 2)), dma((3, 2, 2)),
            dma((2,)), dma((2,)), dma((3, 2)), dma((3, 2)),
            dma((2,)), dma((2,)), dma((2, NZ, 2)), dma((2, NZ, 2)),
            pltpu.SemaphoreType.REGULAR((2,)),
        ],
        compiler_params=pltpu.CompilerParams(
            collective_id=0, has_side_effects=True, vmem_limit_bytes=60 * 1024 * 1024
        ),
        name="whole",
    )(rows, tiles, cols, aux, count, occ, vir)


def widen_kernel(src, dst, narrow, wide, in_sem, out_sem):
    pieces = 8
    width = 16 * PDEV // pieces

    def columns(ref, n):
        return ref.at[:, n * width:(n + 1) * width]

    loads = [pltpu.make_async_copy(columns(src, n), narrow.at[n], in_sem.at[n]) for n in range(pieces)]
    stores = [pltpu.make_async_copy(wide.at[n], columns(dst, n), out_sem.at[n]) for n in range(pieces)]
    for cp in loads:
        cp.start()
    for n in range(pieces):
        loads[n].wait()
        wide[n] = narrow[n].astype(jnp.float32)
        stores[n].start()
    for cp in stores:
        cp.wait()


def widen(result):
    anywhere = pl.BlockSpec(memory_space=pl.ANY)
    return pl.pallas_call(
        widen_kernel,
        out_shape=jax.ShapeDtypeStruct((64, 16 * PDEV), jnp.float32),
        in_specs=[anywhere],
        out_specs=anywhere,
        scratch_shapes=[
            pltpu.VMEM((8, 64, 2 * PDEV), jnp.bfloat16),
            pltpu.VMEM((8, 64, 2 * PDEV), jnp.float32),
            pltpu.SemaphoreType.DMA((8,)),
            pltpu.SemaphoreType.DMA((8,)),
        ],
        name="widen",
    )(result)


def shards(integral_tiles, row_blocks, col_blocks, aux_blocks, tile_counts, occ_coeffs, vir_coeffs):
    result = whole(
        row_blocks.reshape(1, KMAX),
        integral_tiles.reshape(KMAX, PB, BLK, BLK),
        col_blocks.reshape(1, KMAX),
        aux_blocks.reshape(1, KMAX),
        tile_counts,
        occ_coeffs,
        vir_coeffs.reshape(4, BLK, V),
    )
    return widen(result)


def solution(mesh):
    in_specs = (
        P("grp", "aux", None, None, None, None),
        P("grp", "aux", None),
        P("grp", "aux", None),
        P("grp", "aux", None),
        P("grp", "aux"),
        P(None, "grp"),
        P("grp", None),
    )
    out_specs = P(("grp", "aux"), None)
    return jax.shard_map(shards, mesh=mesh, in_specs=in_specs, out_specs=out_specs, check_vma=False)
```
